32 devices in a mesh: row: 8 (over y, x, core), col: 4 (over z).
Axes of the slice: x: 2, y: 2, z: 4, core: 2. Of those that a mesh axis runs over, the one named last changes fastest.
Arguments:
- front_matrix: bfloat16 [20480, 20480], P('row', 'col'), may hold values from -37 to 37
- right_samples: bfloat16 [20480, 256], P('col'), may hold values from -0.0390625 to 0.0390625
- left_samples: bfloat16 [20480, 256], P('row'), may hold values from -0.0390625 to 0.0390625
Outputs:
- residual: bfloat16 [20480, 20480], P('row', 'col')
- core_scaled: float32 [256, 256], replicated
The draws below stay inside these ranges and needn't reach their ends.
All inputs are finite; a program needn't handle non-finite values.
Results may differ from the reference program's by a relative error of at most 0.0035.
Values may be sent and summed in bfloat16 or wider, within the bound.
A program may use at most 128 MiB of HBM per device.

```python
import math
import jax
import jax.numpy as jnp
from jax import lax

ORDER = 20480
SAMPLES = 256
N_ROW = 8


def draw_front_matrix(key, part):
    keys = jax.random.split(jax.random.fold_in(key, 17), 6)
    row_scale = jnp.exp(jax.random.uniform(keys[0], (ORDER,), jnp.float32, math.log(0.05), math.log(0.5)))
    segment = ORDER // 8
    offsets = jax.random.randint(keys[5], (8,), 0, segment)
    heavy_rows = (jnp.arange(8) * segment + offsets).astype(jnp.int32)
    row_scale = row_scale.at[heavy_rows].set(3.0)
    col_scale = jnp.exp(jax.random.uniform(keys[1], (ORDER,), jnp.float32, math.log(0.3), math.log(3.0)))
    base = jnp.clip(jax.random.normal(keys[2], (ORDER, ORDER), jnp.float32), -4.0, 4.0)
    values = base * row_scale[:, None] * col_scale[None, :]
    return values.astype(jnp.bfloat16)


def block_levels(rng, extent, cuts, smallest, high):
    def one(dim, parts):
        draws = jax.random.uniform(jax.random.fold_in(jax.random.fold_in(rng, 6), dim), (parts,), jnp.float32, smallest / len(cuts), high / len(cuts))
        return jnp.repeat(jnp.exp(draws), extent[dim] // parts).reshape((-1,) + (1,) * (len(extent) - dim - 1))

    loudness = one(*cuts[0])
    for cut in cuts[1:]:
        loudness = loudness * one(*cut)
    return loudness


def bell_draw(own_key, dims, spread, most, cuts=(), dtype=jnp.bfloat16):
    gain = block_levels(own_key, dims, cuts, -0.22, 0.18) if cuts else 1.0
    result = jax.random.normal(own_key, dims, jnp.float32) * spread * gain
    return jnp.minimum(jnp.maximum(result, -most), most).astype(dtype)


def setup_inputs(seed: int = 0) -> dict:
    splits = jax.random.split(jax.random.key(seed), 4)
    front_matrix = draw_front_matrix(jax.random.fold_in(splits[3], 71), 0)
    right_samples = bell_draw(splits[1], (ORDER, SAMPLES), ORDER ** -0.5, 0.0390625, ((0, 4),))
    left_samples = bell_draw(splits[2], (ORDER, SAMPLES), ORDER ** -0.5, 0.0390625, ((0, 8),))
    return dict(front_matrix=front_matrix, right_samples=right_samples, left_samples=left_samples)


def orthonormal(sketch):
    gram_matrix = lax.dot_general(sketch.astype(jnp.float32), sketch.astype(jnp.float32), (((0,), (0,)), ((), ())), precision=lax.Precision.HIGHEST, preferred_element_type=jnp.float32)
    lower_factor = jnp.linalg.cholesky(gram_matrix)
    return jax.scipy.linalg.solve_triangular(lower_factor, sketch.T, lower=True).T

def reference(front_matrix, right_samples, left_samples):
    sketch_rows = jnp.dot(front_matrix.astype(jnp.float32), right_samples.astype(jnp.float32), preferred_element_type=jnp.float32)
    sketch_cols = lax.dot_general(front_matrix.astype(jnp.float32), left_samples.astype(jnp.float32), (((0,), (0,)), ((), ())), preferred_element_type=jnp.float32)
    basis_rows = orthonormal(sketch_rows).astype(jnp.bfloat16)
    basis_cols = orthonormal(sketch_cols).astype(jnp.bfloat16)
    applied = jnp.dot(front_matrix.astype(jnp.float32), basis_cols.astype(jnp.float32), preferred_element_type=jnp.float32)
    core_matrix = lax.dot_general(basis_rows.astype(jnp.float32), applied.astype(jnp.float32), (((0,), (0,)), ((), ())), precision=lax.Precision.HIGHEST, preferred_element_type=jnp.float32)
    core_scaled = core_matrix / jnp.sqrt(jnp.float32(ORDER))
    projected = jnp.dot(basis_rows.astype(jnp.float32), core_matrix.astype(jnp.float32), precision=lax.Precision.HIGHEST, preferred_element_type=jnp.float32).astype(jnp.bfloat16)
    row_blocks = front_matrix.reshape(N_ROW, ORDER // N_ROW, ORDER)
    proj_blocks = projected.reshape(N_ROW, ORDER // N_ROW, SAMPLES)

    def update_block(pair):
        block_front, block_proj = pair
        update = lax.dot_general(block_proj.astype(jnp.float32), basis_cols.astype(jnp.float32), (((1,), (1,)), ((), ())), preferred_element_type=jnp.float32)
        return (block_front.astype(jnp.float32) - update).astype(jnp.bfloat16)
    residual = lax.map(update_block, (row_blocks, proj_blocks)).reshape(ORDER, ORDER)
    return (residual, core_scaled)
```

```python
import functools
import math

import jax
import jax.numpy as jnp
from jax import lax
from jax.experimental import pallas as pl
from jax.experimental.pallas import tpu as pltpu
from jax.sharding import PartitionSpec as P

F32 = jnp.float32
BF16 = jnp.bfloat16
BASE = 64
CHUNKS = 10
LAG = 2
RING = 4
MIB = 1024 * 1024


def mm(a, b, dims=((1,), (0,))):
    return lax.dot_general(
        a, b, (dims, ((), ())), precision=lax.Precision.HIGHEST, preferred_element_type=F32
    )


def base_inverse(grams):
    size = grams[0].shape[0]
    tall = size // 8
    width = 2 * size
    eye = (
        lax.broadcasted_iota(jnp.int32, (size, size), 0) == lax.broadcasted_iota(jnp.int32, (size, size), 1)
    ).astype(F32)
    wide = [jnp.concatenate([g, eye], axis=1) for g in grams]
    parts = [[w[8 * t : 8 * t + 8] for t in range(tall)] for w in wide]
    sub = lax.broadcasted_iota(jnp.int32, (8, width), 0)
    for k in range(size):
        top, at = k // 8, k % 8
        for part in parts:
            row = part[top][at : at + 1, :]
            scaled = row * (1.0 / row[:, k : k + 1])
            for t in range(top, tall):
                col = part[t][:, k : k + 1]
                if t == top:
                    if at == 7:
                        continue
                    part[t] = part[t] - jnp.where(sub > at, col * scaled, 0.0)
                else:
                    part[t] = part[t] - col * scaled
    out = []
    for part in parts:
        full = jnp.concatenate(part, axis=0)
        left, right = full[:, :size], full[:, size:]
        pivot = jnp.sum(left * eye, axis=1, keepdims=True)
        out.append(right * lax.rsqrt(pivot))
    return out


def inverse_factors(grams):
    size = grams[0].shape[0]
    if size <= BASE:
        return base_inverse(grams)
    half = size // 2
    first = inverse_factors([g[:half, :half] for g in grams])
    lower = [mm(g[half:, :half], w, ((1,), (1,))) for g, w in zip(grams, first)]
    rest = [g[half:, half:] - mm(l, l, ((1,), (1,))) for g, l in zip(grams, lower)]
    second = inverse_factors(rest)
    out = []
    for w1, l21, w2 in zip(first, lower, second):
        below = -mm(w2, mm(l21, w1))
        out.append(
            jnp.concatenate(
                [
                    jnp.concatenate([w1, jnp.zeros_like(w1)], axis=1),
                    jnp.concatenate([below, w2], axis=1),
                ],
                axis=0,
            )
        )
    return out


def split(x):
    high = x.astype(BF16)
    return high, (x - high.astype(F32)).astype(BF16)


def dot(a, b, dims=((1,), (0,))):
    return lax.dot_general(a, b, (dims, ((), ())), preferred_element_type=F32)


def remote(source, target, send, recv, where):
    return pltpu.make_async_remote_copy(
        src_ref=source,
        dst_ref=target,
        send_sem=send,
        recv_sem=recv,
        device_id=where,
        device_id_type=pl.DeviceIdType.MESH,
    )


def spread(axis, count, source, slots, send, recv):
    me = lax.axis_index(axis)
    copies = []
    for step in range(1, count):
        peer = lax.rem(me + step, count)
        copies.append(remote(source(peer), slots.at[step - 1], send.at[step - 1], recv.at[step - 1], {axis: peer}))
    for copy in copies:
        copy.start()
    return copies


def gather(count, block, send, recv):
    me = lax.axis_index("row")
    sends, receives = [], []
    for step in range(1, count):
        for slot, bag in ((me, sends), (lax.rem(me - step + count, count), receives)):
            peer = {"row": lax.rem(me + step, count)}
            bag.append(remote(block(me), block(slot), send.at[step - 1], recv.at[step - 1], peer))
    for copy in sends:
        copy.start()
    return sends, receives


def sketch_kernel(rows, cols, steps, *refs):
    front, right, left = refs[:3]
    yhi, zt, total = refs[3:6]
    f_ref, r_buf, lt, yown, y_in, y_out, zp, z_core, z_sum, z_in, t_acc, cross, gram, slab, row_buf, own, col_buf = refs[6:23]
    (f_sem, io_sem, core_s, core_r, fin_s, fin_r, ph_s, ph_r, ch_s, ch_r, rs_s, rs_r, cs_s, cs_r, ag_s, ag_r) = refs[23:]
    n = steps
    depth, width = f_ref.shape
    size = yhi.shape[1]
    half = size // 2
    quart = size // 4
    dh, cw = depth // n, width // n
    phases = z_sum.shape[0]
    last = cols - 1
    span = size // rows
    me_r, me_c = lax.axis_index("row"), lax.axis_index("col")
    core = lax.rem(me_r, 2)

    barrier = pltpu.get_barrier_semaphore()
    for axis, count in (("row", rows), ("col", cols)):
        me = lax.axis_index(axis)
        for step in range(1, count):
            pl.semaphore_signal(
                barrier, inc=1, device_id={axis: lax.rem(me + step, count)}, device_id_type=pl.DeviceIdType.MESH
            )

    def shell(k):
        down = (pl.ds(k * dh, depth - k * dh), pl.ds(k * cw, cw))
        out = [pltpu.make_async_copy(front.at[down], f_ref.at[down], f_sem.at[0, k])]
        if k + 1 < n:
            over = (pl.ds(k * dh, dh), pl.ds((k + 1) * cw, width - (k + 1) * cw))
            out.append(pltpu.make_async_copy(front.at[over], f_ref.at[over], f_sem.at[1, k]))
        return out

    load_l = pltpu.make_async_copy(left, yhi, io_sem.at[0])
    load_r = pltpu.make_async_copy(right, r_buf, io_sem.at[1])
    load_l.start()
    first = shell(0)
    first[0].start()
    load_r.start()
    for copy in first[1:] + shell(1):
        copy.start()
    t_acc[...] = jnp.zeros_like(t_acc)
    gram[...] = jnp.zeros_like(gram)
    slab[...] = jnp.zeros_like(slab)
    load_l.wait()

    @pl.loop(0, depth // 128)
    def _(i):
        at = pl.ds(pl.multiple_of(i * 128, 128), 128)
        lt[:, at] = yhi[at, :].astype(F32).T.astype(BF16)

    def flip(bit):
        return {"row": me_r + bit - 2 * bit * lax.rem(lax.div(me_r, bit), 2)}

    bits = [2 << q for q in range(phases)]
    paths = (bits, bits[::-1])

    def cols_of(k):
        return pl.ds(pl.multiple_of(k * cw, cw), cw)

    def rows_of(k):
        return pl.ds(pl.multiple_of(k * dh, dh), dh)

    def core_copy(k):
        slot = lax.rem(k, RING)
        return remote(zp.at[slot, 1 - core], z_core.at[k], core_s.at[k], core_r.at[k], flip(1))

    def phase_copy(q, way, k):
        return remote(
            z_sum.at[q, way, lax.rem(k, RING)], z_in.at[q, way, k], ph_s.at[q, way, k], ph_r.at[q, way, k], flip(paths[way][q])
        )

    def final_copy(k):
        return remote(zt.at[k, core], zt.at[k, core], fin_s.at[k], fin_r.at[k], flip(1))

    def final_wait(k):
        other = zt.at[k, 1 - core]
        remote(other, other, fin_s.at[k], fin_r.at[k], flip(1)).wait_recv()

    def chain_copy(way, k):
        to = lax.rem(me_c + (1 if way == 0 else last), cols)
        return remote(
            y_out.at[way, lax.rem(k, RING)], y_in.at[way, k], ch_s.at[way, k], ch_r.at[way, k], {"col": to}
        )

    def compute(k):
        for s in range(n):

            @pl.when(k == s)
            def _():
                for copy in shell(s):
                    copy.wait()
                if s + 2 < n:
                    for copy in shell(s + 2):
                        copy.start()

        @pl.when(k >= RING)
        def _():
            core_copy(k - RING).wait_send()

        slot = lax.rem(k, RING)
        part = dot(lt[...], f_ref[:, cols_of(k)]).astype(BF16)
        zp[slot, 0] = part[:half]
        zp[slot, 1] = part[half:]

        @pl.when(k == 0)
        def _():
            load_r.wait()

        yown[k] = dot(f_ref[rows_of(k), :], r_buf[...])

    def push_chain(way, k, place, value):
        @pl.when(k >= RING)
        def _():
            chain_copy(way, k - RING).wait_send()

        y_out[way, lax.rem(k, RING)] = value.astype(BF16)
        chain_copy(way, k).start()

    def send_phase(q, k, value):
        @pl.when(k >= RING)
        def _():
            for way in range(2):
                phase_copy(q, way, k - RING).wait_send()

        z_sum[q, 0, lax.rem(k, RING)] = value[:quart]
        z_sum[q, 1, lax.rem(k, RING)] = value[quart:]
        for way in range(2):
            phase_copy(q, way, k).start()

    def arrived(q, k):
        parts = []
        for way in range(2):
            phase_copy(q, way, k).wait_recv()
            parts.append((z_sum[q, way, lax.rem(k, RING)].astype(F32) + z_in[q, way, k].astype(F32)).astype(BF16))
        return jnp.concatenate(parts, axis=0)

    def inside(k, body):
        @pl.when((k >= 0) & (k < n))
        def _():
            body(k)

    compute(0)
    pl.semaphore_wait(barrier, rows + cols - 2)

    z_lag = LAG * phases
    y_lag = LAG * last
    row_tile = math.gcd(depth, 640)

    @pl.loop(0, n + max(z_lag + 1, y_lag))
    def _(t):
        @pl.when(t < n)
        def _():
            core_copy(t).start()
            for way in range(2):
                place = me_c if way == 0 else last - me_c

                @pl.when(place == 0)
                def _():
                    push_chain(way, t, place, yown[t])

        @pl.when(t + 1 < n)
        def _():
            compute(t + 1)

        @pl.when(t < n)
        def _():
            core_copy(t).wait_recv()
            mine = zp[lax.rem(t, RING), core].astype(F32) + z_core[t].astype(F32)
            send_phase(0, t, mine.astype(BF16))

        for q in range(1, phases):
            inside(t - LAG * q, lambda k: send_phase(q, k, arrived(q - 1, k)))

        for way in range(2):
            place = me_c if way == 0 else last - me_c
            k = t - LAG * place

            @pl.when((place > 0) & (k >= 0) & (k < n))
            def _():
                chain_copy(way, k).wait_recv()

                @pl.when(place < last)
                def _():
                    push_chain(way, k, place, yown[k] + y_in[way, k].astype(F32))

        def z_final(k):
            zt[k, core] = arrived(phases - 1, k)
            final_copy(k).start()

        inside(t - z_lag, z_final)

        def y_final(k):
            for way in range(2):
                place = me_c if way == 0 else last - me_c

                @pl.when(place > 0)
                def _():
                    yown[k] = yown[k] + y_in[way, k].astype(F32)

            value = yown[k]
            high, low = split(value)
            yhi[rows_of(k), :] = high

            @pl.when(lax.rem(k, cols) == me_c)
            def _():
                across_high, across_low = split(value.T)
                gram[...] = gram[...] + (dot(across_high, high) + (dot(across_high, low) + dot(across_low, high)))

        inside(t - y_lag, y_final)

        def z_use(k):
            final_wait(k)
            block = zt[k].reshape(size, cw)
            at = me_r * span
            piece = zt[k, lax.div(at, half), pl.ds(pl.multiple_of(lax.rem(at, half), span), span), :]
            slab[...] = slab[...] + dot(piece, block, ((1,), (1,)))

            @pl.loop(0, depth // row_tile)
            def _(i):
                at = pl.ds(pl.multiple_of(i * row_tile, row_tile), row_tile)
                t_acc[at, :] = t_acc[at, :] + dot(f_ref[at, cols_of(k)], block, ((1,), (1,)))

        inside(t - z_lag - 1, z_use)

    def piece_of(ref):
        return lambda k: ref.at[pl.ds(pl.multiple_of(k * span, span), span), :]

    def row_sum(m, ref, copies):
        for copy in copies:
            copy.wait()
        value = piece_of(ref)(me_r)[...]
        for step in range(rows - 1):
            value = value + row_buf[m, step]
        return value

    def col_send(m, value):
        own[m] = value
        col_buf[m, cols - 1] = value
        return spread("col", cols, lambda k: own.at[m], col_buf.at[m], cs_s.at[m], cs_r.at[m])

    def col_sum(m, copies):
        for copy in copies:
            copy.wait()
        value = None
        for member in range(cols):
            slot = lax.rem(me_c - member + 2 * cols - 1, cols)
            value = col_buf[m, slot] if value is None else value + col_buf[m, slot]
        total[me_r, m] = value
        return gather(rows, lambda k: total.at[k, m], ag_s.at[m], ag_r.at[m])

    gram_rows = spread("row", rows, piece_of(gram), row_buf.at[0], rs_s.at[0], rs_r.at[0])
    slab_cols = col_send(2, slab[...])
    cross[...] = jnp.zeros_like(cross)

    @pl.loop(0, n)
    def _(k):
        high, low = split(t_acc[rows_of(k), :])
        across_high, across_low = split(yown[k].T)
        cross[...] = cross[...] + (dot(across_high, high) + (dot(across_high, low) + dot(across_low, high)))

    cross_rows = spread("row", rows, piece_of(cross), row_buf.at[1], rs_s.at[1], rs_r.at[1])
    gram_cols = col_send(0, row_sum(0, gram, gram_rows))
    slab_all = col_sum(2, slab_cols)
    cross_cols = col_send(1, row_sum(1, cross, cross_rows))
    gram_all = col_sum(0, gram_cols)
    cross_all = col_sum(1, cross_cols)

    @pl.loop(0, n)
    def _(k):
        final_copy(k).wait_send()

    @pl.loop(max(n - RING, 0), n)
    def _(k):
        core_copy(k).wait_send()
        for q in range(phases):
            for way in range(2):
                phase_copy(q, way, k).wait_send()
        for way in range(2):
            place = me_c if way == 0 else last - me_c

            @pl.when(place < last)
            def _():
                chain_copy(way, k).wait_send()

    for sends, receives in (slab_all, gram_all, cross_all):
        for copy in receives:
            copy.wait_recv()
        for copy in sends:
            copy.wait_send()


def sketch(front, right, left, rows, cols):
    depth, width = front.shape
    size = right.shape[1]
    n = CHUNKS
    while width % (128 * n) or depth % (16 * n):
        n -= 1
    phases = rows.bit_length() - 2
    half, quart, span = size // 2, size // 4, size // rows
    dh, cw = depth // n, width // n
    dma = pltpu.SemaphoreType.DMA
    vmem = pl.BlockSpec(memory_space=pltpu.VMEM)
    hbm = pl.BlockSpec(memory_space=pl.ANY)
    return pl.pallas_call(
        functools.partial(sketch_kernel, rows, cols, n),
        out_shape=(
            pltpu.VMEM((depth, size), BF16),
            pltpu.VMEM((n, 2, half, cw), BF16),
            pltpu.VMEM((rows, 3, span, size), F32),
        ),
        in_specs=[hbm] * 3,
        out_specs=(vmem,) * 3,
        scratch_shapes=[
            pltpu.VMEM((depth, width), BF16),
            pltpu.VMEM((width, size), BF16),
            pltpu.VMEM((size, depth), BF16),
            pltpu.VMEM((n, dh, size), F32),
            pltpu.VMEM((2, n, dh, size), BF16),
            pltpu.VMEM((2, RING, dh, size), BF16),
            pltpu.VMEM((RING, 2, half, cw), BF16),
            pltpu.VMEM((n, half, cw), BF16),
            pltpu.VMEM((phases, 2, RING, quart, cw), BF16),
            pltpu.VMEM((phases, 2, n, quart, cw), BF16),
            pltpu.VMEM((depth, size), F32),
            pltpu.VMEM((size, size), F32),
            pltpu.VMEM((size, size), F32),
            pltpu.VMEM((span, size), F32),
            pltpu.VMEM((2, rows - 1, span, size), F32),
            pltpu.VMEM((3, span, size), F32),
            pltpu.VMEM((3, cols, span, size), F32),
            dma((2, n)),
            dma((2,)),
            dma((n,)),
            dma((n,)),
            dma((n,)),
            dma((n,)),
            dma((phases, 2, n)),
            dma((phases, 2, n)),
            dma((2, n)),
            dma((2, n)),
            dma((2, rows - 1)),
            dma((2, rows - 1)),
            dma((3, cols - 1)),
            dma((3, cols - 1)),
            dma((3, rows - 1)),
            dma((3, rows - 1)),
        ],
        compiler_params=pltpu.CompilerParams(collective_id=0, has_side_effects=True, vmem_limit_bytes=58 * MIB),
    )(front, right, left)


def finish_kernel(order, tile, front, total_ref, y_ref, z_ref, out_ref, core_ref, f_ref, p_ref, in_sem, out_sem):
    load = pltpu.make_async_copy(front, f_ref, in_sem)
    load.start()
    size = core_ref.shape[0]
    depth = f_ref.shape[0]
    n, _, _, cw = z_ref.shape
    gram_r, cross, gram_c = (total_ref[:, m].reshape(size, size) for m in range(3))
    w_r, w_c = inverse_factors([gram_r, gram_c])
    core = mm(mm(w_r, cross), w_c, ((1,), (1,)))
    core_ref[...] = core / jnp.sqrt(F32(order))
    high, low = split(mm(mm(w_r, core, ((0,), (0,))), w_c))
    p_ref[...] = (dot(y_ref[...], high) + dot(y_ref[...], low)).astype(BF16)
    load.wait()
    per = depth // tile

    def spot(i):
        at = pl.ds(pl.multiple_of(lax.rem(i, per) * tile, 16), tile)
        return at, pl.ds(pl.multiple_of(lax.div(i, per) * cw, 128), cw)

    def store(i):
        at, cols = spot(i)
        return pltpu.make_async_copy(f_ref.at[at, cols], out_ref.at[at, cols], out_sem.at[i])

    @pl.loop(0, n * per)
    def _(i):
        at, cols = spot(i)
        update = dot(p_ref[at, :], z_ref[lax.div(i, per)].reshape(size, cw))
        f_ref[at, cols] = (f_ref[at, cols].astype(F32) - update).astype(BF16)
        store(i).start()

    @pl.loop(0, n * per)
    def _(i):
        store(i).wait()


def finish(front, total, y, z, order):
    depth, width = front.shape
    size = y.shape[1]
    n = z.shape[0]
    tile = math.gcd(depth, 1280)
    vmem = pl.BlockSpec(memory_space=pltpu.VMEM)
    hbm = pl.BlockSpec(memory_space=pl.ANY)
    return pl.pallas_call(
        functools.partial(finish_kernel, order, tile),
        out_shape=(jax.ShapeDtypeStruct((depth, width), BF16), jax.ShapeDtypeStruct((size, size), F32)),
        in_specs=[hbm, vmem, vmem, vmem],
        out_specs=(hbm, vmem),
        scratch_shapes=[
            pltpu.VMEM((depth, width), BF16),
            pltpu.VMEM((depth, size), BF16),
            pltpu.SemaphoreType.DMA,
            pltpu.SemaphoreType.DMA((n * (depth // tile),)),
        ],
        compiler_params=pltpu.CompilerParams(vmem_limit_bytes=36 * MIB),
    )(front, total, y, z)


def body(order, rows, cols, front, right, left):
    y, z, total = sketch(front, right, left, rows, cols)
    return finish(front, total, y, z, order)


def solution(mesh):
    in_specs = (P("row", "col"), P("col", None), P("row", None))
    out_specs = (P("row", "col"), P())

    def run(front, right, left):
        inner = functools.partial(body, front.shape[0], mesh.shape["row"], mesh.shape["col"])
        return jax.shard_map(inner, mesh=mesh, in_specs=in_specs, out_specs=out_specs, check_vma=False)(
            front, right, left
        )

    return run
```

```python
import functools
import math

import jax
import jax.numpy as jnp
from jax import lax
from jax.experimental import pallas as pl
from jax.experimental.pallas import tpu as pltpu
from jax.sharding import PartitionSpec as P

F32 = jnp.float32
BF16 = jnp.bfloat16
BASE = 64
CHUNKS = 10
LAG = 2
RING = 4
MIB = 1024 * 1024


def mm(a, b, dims=((1,), (0,))):
    return lax.dot_general(
        a, b, (dims, ((), ())), precision=lax.Precision.HIGHEST, preferred_element_type=F32
    )


def base_inverse(grams):
    size = grams[0].shape[0]
    tall = size // 8
    width = 2 * size
    eye = (lax.broadcasted_iota(jnp.int32, (size, size), 0) == lax.broadcasted_iota(jnp.int32, (size, size), 1)).astype(F32)
    wide = [jnp.concatenate([g, eye], axis=1) for g in grams]
    parts = [[w[8 * t : 8 * t + 8] for t in range(tall)] for w in wide]
    sub = lax.broadcasted_iota(jnp.int32, (8, width), 0)
    out = [[] for _ in grams]
    for p in range(tall):
        for part, done in zip(parts, out):
            block = part[p]
            cols = [jnp.broadcast_to(block[:, 8 * p + j : 8 * p + j + 1], (8, width)) for j in range(8)]
            side = [[jnp.broadcast_to(part[t][:, 8 * p + j : 8 * p + j + 1], (8, width)) for j in range(8)] for t in range(p + 1, tall)]
            keep = block
            for k in range(8):
                inverse = 1.0 / cols[k][k : k + 1, :]
                pivot_row = block[k : k + 1, :]
                keep = jnp.where(sub == k, pivot_row * lax.rsqrt(cols[k][k : k + 1, :]), keep)
                scaled = pivot_row * inverse
                column = cols[k]
                block = jnp.where(sub == k, scaled, block - column * scaled)
                for j in range(k + 1, 8):
                    ratio = cols[j][k : k + 1, :] * inverse
                    cols[j] = jnp.where(sub == k, ratio, cols[j] - column * ratio)
            done.append(keep)
            for s, t in zip(side, range(p + 1, tall)):
                acc = part[t]
                for k in range(8):
                    acc = acc - s[k] * block[k : k + 1, :]
                part[t] = acc
    return [jnp.concatenate(done, axis=0)[:, size:] for done in out]


def inverse_factors(grams):
    size = grams[0].shape[0]
    if size <= BASE:
        return base_inverse(grams)
    half = size // 2
    first = inverse_factors([g[:half, :half] for g in grams])
    lower = [mm(g[half:, :half], w, ((1,), (1,))) for g, w in zip(grams, first)]
    rest = [g[half:, half:] - mm(l, l, ((1,), (1,))) for g, l in zip(grams, lower)]
    second = inverse_factors(rest)
    out = []
    for w1, l21, w2 in zip(first, lower, second):
        below = -mm(w2, mm(l21, w1))
        out.append(
            jnp.concatenate(
                [
                    jnp.concatenate([w1, jnp.zeros_like(w1)], axis=1),
                    jnp.concatenate([below, w2], axis=1),
                ],
                axis=0,
            )
        )
    return out


def split(x):
    high = x.astype(BF16)
    return high, (x - high.astype(F32)).astype(BF16)


def dot(a, b, dims=((1,), (0,))):
    return lax.dot_general(a, b, (dims, ((), ())), preferred_element_type=F32)


def remote(source, target, send, recv, where):
    return pltpu.make_async_remote_copy(
        src_ref=source,
        dst_ref=target,
        send_sem=send,
        recv_sem=recv,
        device_id=where,
        device_id_type=pl.DeviceIdType.MESH,
    )


def spread(axis, count, source, slots, send, recv):
    me = lax.axis_index(axis)
    copies = []
    for step in range(1, count):
        peer = lax.rem(me + step, count)
        copies.append(remote(source(peer), slots.at[step - 1], send.at[step - 1], recv.at[step - 1], {axis: peer}))
    for copy in copies:
        copy.start()
    return copies


def gather(count, block, send, recv):
    me = lax.axis_index("row")
    sends, receives = [], []
    for step in range(1, count):
        for slot, bag in ((me, sends), (lax.rem(me - step + count, count), receives)):
            peer = {"row": lax.rem(me + step, count)}
            bag.append(remote(block(me), block(slot), send.at[step - 1], recv.at[step - 1], peer))
    for copy in sends:
        copy.start()
    return sends, receives


def sketch_kernel(rows, cols, steps, *refs):
    front, right, left = refs[:3]
    yhi, zt, total = refs[3:6]
    f_ref, r_buf, lt, yown, y_in, y_out, zp, z_core, z_sum, z_in, t_acc, cross, gram, slab, row_buf, own, col_buf = refs[6:23]
    (f_sem, io_sem, core_s, core_r, fin_s, fin_r, ph_s, ph_r, ch_s, ch_r, rs_s, rs_r, cs_s, cs_r, ag_s, ag_r) = refs[23:]
    n = steps
    depth, width = f_ref.shape
    size = yhi.shape[1]
    half = size // 2
    quart = size // 4
    dh, cw = depth // n, width // n
    phases = z_sum.shape[0]
    last = cols - 1
    span = size // rows
    me_r, me_c = lax.axis_index("row"), lax.axis_index("col")
    core = lax.rem(me_r, 2)

    barrier = pltpu.get_barrier_semaphore()
    for axis, count in (("row", rows), ("col", cols)):
        me = lax.axis_index(axis)
        for step in range(1, count):
            pl.semaphore_signal(
                barrier, inc=1, device_id={axis: lax.rem(me + step, count)}, device_id_type=pl.DeviceIdType.MESH
            )

    def shell(k):
        down = (pl.ds(k * dh, depth - k * dh), pl.ds(k * cw, cw))
        out = [pltpu.make_async_copy(front.at[down], f_ref.at[down], f_sem.at[0, k])]
        if k + 1 < n:
            over = (pl.ds(k * dh, dh), pl.ds((k + 1) * cw, width - (k + 1) * cw))
            out.append(pltpu.make_async_copy(front.at[over], f_ref.at[over], f_sem.at[1, k]))
        return out

    load_l = pltpu.make_async_copy(left, yhi, io_sem.at[0])
    load_r = pltpu.make_async_copy(right, r_buf, io_sem.at[1])
    load_l.start()
    first = shell(0)
    first[0].start()
    load_r.start()
    for copy in first[1:] + shell(1):
        copy.start()
    t_acc[...] = jnp.zeros_like(t_acc)
    gram[...] = jnp.zeros_like(gram)
    slab[...] = jnp.zeros_like(slab)
    load_l.wait()

    @pl.loop(0, depth // 128)
    def _(i):
        at = pl.ds(pl.multiple_of(i * 128, 128), 128)
        lt[:, at] = yhi[at, :].astype(F32).T.astype(BF16)

    def flip(bit):
        return {"row": me_r + bit - 2 * bit * lax.rem(lax.div(me_r, bit), 2)}

    bits = [2 << q for q in range(phases)]
    paths = (bits, bits[::-1])

    def cols_of(k):
        return pl.ds(pl.multiple_of(k * cw, cw), cw)

    def rows_of(k):
        return pl.ds(pl.multiple_of(k * dh, dh), dh)

    def core_copy(k):
        slot = lax.rem(k, RING)
        return remote(zp.at[slot, 1 - core], z_core.at[k], core_s.at[k], core_r.at[k], flip(1))

    def phase_copy(q, way, k):
        return remote(
            z_sum.at[q, way, lax.rem(k, RING)], z_in.at[q, way, k], ph_s.at[q, way, k], ph_r.at[q, way, k], flip(paths[way][q])
        )

    def final_copy(k):
        return remote(zt.at[k, core], zt.at[k, core], fin_s.at[k], fin_r.at[k], flip(1))

    def final_wait(k):
        other = zt.at[k, 1 - core]
        remote(other, other, fin_s.at[k], fin_r.at[k], flip(1)).wait_recv()

    def chain_copy(way, k):
        to = lax.rem(me_c + (1 if way == 0 else last), cols)
        return remote(
            y_out.at[way, lax.rem(k, RING)], y_in.at[way, k], ch_s.at[way, k], ch_r.at[way, k], {"col": to}
        )

    def compute(k):
        for s in range(n):

            @pl.when(k == s)
            def _():
                for copy in shell(s):
                    copy.wait()
                if s + 2 < n:
                    for copy in shell(s + 2):
                        copy.start()

        @pl.when(k >= RING)
        def _():
            core_copy(k - RING).wait_send()

        slot = lax.rem(k, RING)
        part = dot(lt[...], f_ref[:, cols_of(k)]).astype(BF16)
        zp[slot, 0] = part[:half]
        zp[slot, 1] = part[half:]

        @pl.when(k == 0)
        def _():
            load_r.wait()

        yown[k] = dot(f_ref[rows_of(k), :], r_buf[...])

    def push_chain(way, k, place, value):
        @pl.when(k >= RING)
        def _():
            chain_copy(way, k - RING).wait_send()

        y_out[way, lax.rem(k, RING)] = value.astype(BF16)
        chain_copy(way, k).start()

    def send_phase(q, k, value):
        @pl.when(k >= RING)
        def _():
            for way in range(2):
                phase_copy(q, way, k - RING).wait_send()

        z_sum[q, 0, lax.rem(k, RING)] = value[:quart]
        z_sum[q, 1, lax.rem(k, RING)] = value[quart:]
        for way in range(2):
            phase_copy(q, way, k).start()

    def arrived(q, k):
        parts = []
        for way in range(2):
            phase_copy(q, way, k).wait_recv()
            parts.append((z_sum[q, way, lax.rem(k, RING)].astype(F32) + z_in[q, way, k].astype(F32)).astype(BF16))
        return jnp.concatenate(parts, axis=0)

    def inside(k, body):
        @pl.when((k >= 0) & (k < n))
        def _():
            body(k)

    compute(0)
    pl.semaphore_wait(barrier, rows + cols - 2)

    z_lag = LAG * phases
    y_lag = LAG * last
    row_tile = math.gcd(depth, 640)

    @pl.loop(0, n + max(z_lag + 1, y_lag))
    def _(t):
        @pl.when(t < n)
        def _():
            core_copy(t).start()
            for way in range(2):
                place = me_c if way == 0 else last - me_c

                @pl.when(place == 0)
                def _():
                    push_chain(way, t, place, yown[t])

        @pl.when(t + 1 < n)
        def _():
            compute(t + 1)

        @pl.when(t < n)
        def _():
            core_copy(t).wait_recv()
            mine = zp[lax.rem(t, RING), core].astype(F32) + z_core[t].astype(F32)
            send_phase(0, t, mine.astype(BF16))

        for q in range(1, phases):
            inside(t - LAG * q, lambda k: send_phase(q, k, arrived(q - 1, k)))

        for way in range(2):
            place = me_c if way == 0 else last - me_c
            k = t - LAG * place

            @pl.when((place > 0) & (k >= 0) & (k < n))
            def _():
                chain_copy(way, k).wait_recv()

                @pl.when(place < last)
                def _():
                    push_chain(way, k, place, yown[k] + y_in[way, k].astype(F32))

        def z_final(k):
            zt[k, core] = arrived(phases - 1, k)
            final_copy(k).start()

        inside(t - z_lag, z_final)

        def y_final(k):
            for way in range(2):
                place = me_c if way == 0 else last - me_c

                @pl.when(place > 0)
                def _():
                    yown[k] = yown[k] + y_in[way, k].astype(F32)

            value = yown[k]
            high, low = split(value)
            yhi[rows_of(k), :] = high

            @pl.when(lax.rem(k, cols) == me_c)
            def _():
                across_high, across_low = split(value.T)
                gram[...] = gram[...] + (dot(across_high, high) + (dot(across_high, low) + dot(across_low, high)))

        inside(t - y_lag, y_final)

        def z_use(k):
            final_wait(k)
            block = zt[k].reshape(size, cw)
            at = me_r * span
            piece = zt[k, lax.div(at, half), pl.ds(pl.multiple_of(lax.rem(at, half), span), span), :]
            slab[...] = slab[...] + dot(piece, block, ((1,), (1,)))

            @pl.loop(0, depth // row_tile)
            def _(i):
                at = pl.ds(pl.multiple_of(i * row_tile, row_tile), row_tile)
                t_acc[at, :] = t_acc[at, :] + dot(f_ref[at, cols_of(k)], block, ((1,), (1,)))

        inside(t - z_lag - 1, z_use)

    def piece_of(ref):
        return lambda k: ref.at[pl.ds(pl.multiple_of(k * span, span), span), :]

    def row_sum(m, ref, copies):
        for copy in copies:
            copy.wait()
        value = piece_of(ref)(me_r)[...]
        for step in range(rows - 1):
            value = value + row_buf[m, step]
        return value

    def col_send(m, value):
        own[m] = value
        col_buf[m, cols - 1] = value
        return spread("col", cols, lambda k: own.at[m], col_buf.at[m], cs_s.at[m], cs_r.at[m])

    def col_sum(m, copies):
        for copy in copies:
            copy.wait()
        value = None
        for member in range(cols):
            slot = lax.rem(me_c - member + 2 * cols - 1, cols)
            value = col_buf[m, slot] if value is None else value + col_buf[m, slot]
        total[me_r, m] = value
        return gather(rows, lambda k: total.at[k, m], ag_s.at[m], ag_r.at[m])

    gram_rows = spread("row", rows, piece_of(gram), row_buf.at[0], rs_s.at[0], rs_r.at[0])
    slab_cols = col_send(2, slab[...])
    cross[...] = jnp.zeros_like(cross)

    @pl.loop(0, n)
    def _(k):
        high, low = split(t_acc[rows_of(k), :])
        across_high, across_low = split(yown[k].T)
        cross[...] = cross[...] + (dot(across_high, high) + (dot(across_high, low) + dot(across_low, high)))

    cross_rows = spread("row", rows, piece_of(cross), row_buf.at[1], rs_s.at[1], rs_r.at[1])
    gram_cols = col_send(0, row_sum(0, gram, gram_rows))
    slab_all = col_sum(2, slab_cols)
    cross_cols = col_send(1, row_sum(1, cross, cross_rows))
    gram_all = col_sum(0, gram_cols)
    cross_all = col_sum(1, cross_cols)

    @pl.loop(0, n)
    def _(k):
        final_copy(k).wait_send()

    @pl.loop(max(n - RING, 0), n)
    def _(k):
        core_copy(k).wait_send()
        for q in range(phases):
            for way in range(2):
                phase_copy(q, way, k).wait_send()
        for way in range(2):
            place = me_c if way == 0 else last - me_c

            @pl.when(place < last)
            def _():
                chain_copy(way, k).wait_send()

    for sends, receives in (slab_all, gram_all, cross_all):
        for copy in receives:
            copy.wait_recv()
        for copy in sends:
            copy.wait_send()


def sketch(front, right, left, rows, cols):
    depth, width = front.shape
    size = right.shape[1]
    n = CHUNKS
    while width % (128 * n) or depth % (16 * n):
        n -= 1
    phases = rows.bit_length() - 2
    half, quart, span = size // 2, size // 4, size // rows
    dh, cw = depth // n, width // n
    dma = pltpu.SemaphoreType.DMA
    vmem = pl.BlockSpec(memory_space=pltpu.VMEM)
    hbm = pl.BlockSpec(memory_space=pl.ANY)
    return pl.pallas_call(
        functools.partial(sketch_kernel, rows, cols, n),
        out_shape=(
            pltpu.VMEM((depth, size), BF16),
            pltpu.VMEM((n, 2, half, cw), BF16),
            pltpu.VMEM((rows, 3, span, size), F32),
        ),
        in_specs=[hbm] * 3,
        out_specs=(vmem,) * 3,
        scratch_shapes=[
            pltpu.VMEM((depth, width), BF16),
            pltpu.VMEM((width, size), BF16),
            pltpu.VMEM((size, depth), BF16),
            pltpu.VMEM((n, dh, size), F32),
            pltpu.VMEM((2, n, dh, size), BF16),
            pltpu.VMEM((2, RING, dh, size), BF16),
            pltpu.VMEM((RING, 2, half, cw), BF16),
            pltpu.VMEM((n, half, cw), BF16),
            pltpu.VMEM((phases, 2, RING, quart, cw), BF16),
            pltpu.VMEM((phases, 2, n, quart, cw), BF16),
            pltpu.VMEM((depth, size), F32),
            pltpu.VMEM((size, size), F32),
            pltpu.VMEM((size, size), F32),
            pltpu.VMEM((span, size), F32),
            pltpu.VMEM((2, rows - 1, span, size), F32),
            pltpu.VMEM((3, span, size), F32),
            pltpu.VMEM((3, cols, span, size), F32),
            dma((2, n)),
            dma((2,)),
            dma((n,)),
            dma((n,)),
            dma((n,)),
            dma((n,)),
            dma((phases, 2, n)),
            dma((phases, 2, n)),
            dma((2, n)),
            dma((2, n)),
            dma((2, rows - 1)),
            dma((2, rows - 1)),
            dma((3, cols - 1)),
            dma((3, cols - 1)),
            dma((3, rows - 1)),
            dma((3, rows - 1)),
        ],
        compiler_params=pltpu.CompilerParams(collective_id=0, has_side_effects=True, vmem_limit_bytes=58 * MIB),
    )(front, right, left)


def finish_kernel(order, tile, front, total_ref, y_ref, z_ref, out_ref, core_ref, f_ref, p_ref, in_sem, out_sem):
    load = pltpu.make_async_copy(front, f_ref, in_sem)
    load.start()
    size = core_ref.shape[0]
    depth = f_ref.shape[0]
    n, _, _, cw = z_ref.shape
    gram_r, cross, gram_c = (total_ref[:, m].reshape(size, size) for m in range(3))
    w_r, w_c = inverse_factors([gram_r, gram_c])
    core = mm(mm(w_r, cross), w_c, ((1,), (1,)))
    core_ref[...] = core / jnp.sqrt(F32(order))
    high, low = split(mm(mm(w_r, core, ((0,), (0,))), w_c))
    p_ref[...] = (dot(y_ref[...], high) + dot(y_ref[...], low)).astype(BF16)
    load.wait()
    per = depth // tile

    def spot(i):
        at = pl.ds(pl.multiple_of(lax.rem(i, per) * tile, 16), tile)
        return at, pl.ds(pl.multiple_of(lax.div(i, per) * cw, 128), cw)

    def store(i):
        at, cols = spot(i)
        return pltpu.make_async_copy(f_ref.at[at, cols], out_ref.at[at, cols], out_sem.at[i])

    @pl.loop(0, n * per)
    def _(i):
        at, cols = spot(i)
        update = dot(p_ref[at, :], z_ref[lax.div(i, per)].reshape(size, cw))
        f_ref[at, cols] = (f_ref[at, cols].astype(F32) - update).astype(BF16)
        store(i).start()

    @pl.loop(0, n * per)
    def _(i):
        store(i).wait()


def finish(front, total, y, z, order):
    depth, width = front.shape
    size = y.shape[1]
    n = z.shape[0]
    tile = math.gcd(depth, 2560)
    vmem = pl.BlockSpec(memory_space=pltpu.VMEM)
    hbm = pl.BlockSpec(memory_space=pl.ANY)
    return pl.pallas_call(
        functools.partial(finish_kernel, order, tile),
        out_shape=(jax.ShapeDtypeStruct((depth, width), BF16), jax.ShapeDtypeStruct((size, size), F32)),
        in_specs=[hbm, vmem, vmem, vmem],
        out_specs=(hbm, vmem),
        scratch_shapes=[
            pltpu.VMEM((depth, width), BF16),
            pltpu.VMEM((depth, size), BF16),
            pltpu.SemaphoreType.DMA,
            pltpu.SemaphoreType.DMA((n * (depth // tile),)),
        ],
        compiler_params=pltpu.CompilerParams(vmem_limit_bytes=36 * MIB),
    )(front, total, y, z)


def body(order, rows, cols, front, right, left):
    y, z, total = sketch(front, right, left, rows, cols)
    return finish(front, total, y, z, order)


def solution(mesh):
    in_specs = (P("row", "col"), P("col", None), P("row", None))
    out_specs = (P("row", "col"), P())

    def run(front, right, left):
        inner = functools.partial(body, front.shape[0], mesh.shape["row"], mesh.shape["col"])
        return jax.shard_map(inner, mesh=mesh, in_specs=in_specs, out_specs=out_specs, check_vma=False)(
            front, right, left
        )

    return run
```
